32 devices in a mesh: fsdp: 16 (over z, x, core), dp: 2 (over y).
Axes of the slice: x: 2, y: 2, z: 4, core: 2. Of those that a mesh axis runs over, the one named last changes fastest.
Arguments:
- tokens: bfloat16 [4096, 4096], P(('fsdp', 'dp')), may hold values from -6 to 6
- owner: int32 [4096, 4], P(('fsdp', 'dp')), may hold values from 0 to 15, all different within a row; in each aligned block of 128 rows (0 to 127, 128 to 255, ...) at most 48 rows name the same one
- row_pick: int32 [4096, 4, 32], P(('fsdp', 'dp')), may hold values from 0 to 255, as said below
- query_weight: bfloat16 [4096, 512], P('fsdp'), may hold values from -0.09375 to 0.09375
- sub_keys: bfloat16 [4, 256, 128], replicated, may hold values from -2000 to 2000
- values: bfloat16 [4096, 4096], P('fsdp'), may hold values from -6 to 6
- cotangent: bfloat16 [4096, 4096], P(('fsdp', 'dp')), may hold values from -6 to 6
Outputs:
- memory_out: bfloat16 [4096, 4096], P(('fsdp', 'dp'))
- grad_values: bfloat16 [4096, 4096], P(('fsdp', 'dp'))
The draws below stay inside these ranges and needn't reach their ends.
Inputs may be any that keep to these rules, and one draw needn't show every extreme that they name: `owner`: each token's 4 heads name different blocks; the 128 tokens of one device name no block more than 48 times, and some block exactly 48 times. `row_pick`: the 32 rows that one head of one token reads are distinct.
All inputs are finite; a program needn't handle non-finite values.
Results may differ from the reference program's by a relative error of at most 0.012.
The reference program's roundings to bfloat16 on the way (of `query`, `weight` and `read`) count: a program that leaves them out, or rounds other values in their place, can miss the bound.
Values may be sent and summed in bfloat16 or wider, within the bound.
A program may use at most 64 MiB of HBM per device.

```python
import math
import jax
import jax.numpy as jnp
import numpy as np
from jax import lax

D = 4096
HEADS = 4
TOPK = 32
KH = 128
VROWS_DEV = 256
TOK_DEV = 128
CAP = 48
TOKENS = 4096
SLAB_ROWS = 4096
N_FSDP = 16


def draw_row_pick(key, part):
    scores = jax.random.randint(key, (TOKENS, HEADS, VROWS_DEV), 0, 2 ** 30)
    order = jnp.argsort(scores, axis=-1, stable=True)
    return order[..., :TOPK].astype(jnp.int32)


def draw_sub_keys(key, part):
    first = jax.random.fold_in(jax.random.fold_in(key, 17), 0)
    base = jax.random.normal(first, (HEADS, VROWS_DEV, KH), jnp.float32)
    base = jnp.clip(base, -6.0, 6.0)
    return base.astype(jnp.bfloat16)


def shard_levels(stream_key, extent, cuts, low, largest):
    def one(position, parts):
        steps = jax.random.uniform(jax.random.fold_in(jax.random.fold_in(stream_key, 6), position), (parts,), jnp.float32, low / len(cuts), largest / len(cuts))
        return jnp.repeat(jnp.exp(steps), extent[position] // parts).reshape((-1,) + (1,) * (len(extent) - position - 1))

    loudness = one(*cuts[0])
    for cut in cuts[1:]:
        loudness = loudness * one(*cut)
    return loudness


def routed_block(own_key, own, number, rows, number_of, top, reach, slope):
    order = jax.random.permutation(own_key, number_of)
    heavy_load, ordinary = load_shares(number_of, rows * top, reach, slope, True), load_shares(number_of, rows * top, reach, slope, False)
    places = jnp.arange(number_of)

    def named(tallies, turn):
        used = int((tallies > 0).sum())
        fixed = max(1, used // 4)
        shifted = fixed + (places - fixed + turn * (used - fixed)) % max(1, number_of - fixed)
        return jnp.zeros((number_of,), jnp.int32).at[order[jnp.where(places < fixed, places, shifted)]].set(jnp.asarray(tallies, jnp.int32))

    tallies = jnp.where(number % 4 == 0, named(heavy_load, number // 4), named(ordinary, number - number // 4 - 1))
    mixed = jax.random.permutation(jax.random.fold_in(own, 3), number_of)
    donor, sink = mixed[0:number_of // 2 * 2:2], mixed[1:number_of // 2 * 2:2]
    slack = jnp.minimum(tallies[donor] - 1, reach - tallies[sink]) // 2
    slack = jnp.where((donor == order[0]) | (sink == order[0]) | (tallies[sink] == 0), 0, jnp.maximum(slack, 0))
    shifted = jax.random.randint(jax.random.fold_in(own, 4), (number_of // 2,), 0, 1 << 20) % (slack + 1)
    tallies = tallies.at[donor].add(-shifted).at[sink].add(shifted)
    labels = jnp.searchsorted(jnp.cumsum(tallies), jnp.arange(rows * top), side="right").astype(jnp.int32)
    listing = labels.reshape(top, rows).T
    listing = listing[jax.random.permutation(jax.random.fold_in(own, 1), rows)]
    turn = jax.random.randint(jax.random.fold_in(own, 2), (rows, 1), 0, top)
    return jnp.take_along_axis(listing, (jnp.arange(top)[None, :] + turn) % top, axis=1)


def load_shares(amount, total, limit, lean, full):
    portions = [(1 << 20) // math.isqrt(grade ** lean) + 1 for grade in range(1, amount + 1)]
    largest = limit if full else min(limit, max(-(-total // amount), total * portions[0] // sum(portions)))
    least = 1 if total - largest >= amount - 1 else 0
    holding, spare = [largest] + [least] * (amount - 1), total - largest - least * (amount - 1)
    while spare > 0:
        free = [i for i in range(1, amount) if holding[i] < largest] or [i for i in range(1, amount) if holding[i] < limit]
        whole, budget = sum([portions[i] for i in free]), spare
        for i in free:
            addition = min(limit - holding[i], max(1, budget * portions[i] // whole), spare)
            holding[i] = holding[i] + addition
            spare = spare - addition
    return np.array(holding)


def scatter_about(rng, shape, spread, bound, cuts=(), held_as=jnp.bfloat16):
    level = shard_levels(rng, shape, cuts, -0.22, 0.18) if cuts else 1.0
    array = jax.random.normal(rng, shape, jnp.float32) * spread * level
    return jnp.minimum(jnp.maximum(array, -bound), bound).astype(held_as)


def setup_inputs(seed: int = 0) -> dict:
    arg_keys = jax.random.split(jax.random.key(seed), 8)
    tokens = scatter_about(arg_keys[0], (TOKENS, D), 1.0, 6.0, ((0, 32),))
    owner_keys = jax.random.split(jax.random.fold_in(arg_keys[1], 1), TOKENS // TOK_DEV)
    owner_turns = jax.random.permutation(jax.random.fold_in(arg_keys[1], 3), TOKENS // TOK_DEV)
    owner = jax.vmap(lambda own, number: routed_block(jax.random.fold_in(arg_keys[1], 2), own, number, TOK_DEV, N_FSDP, HEADS, CAP, 2))(owner_keys, owner_turns).reshape((TOKENS, HEADS))
    row_pick = draw_row_pick(jax.random.fold_in(arg_keys[7], 71), 0)
    query_weight = scatter_about(arg_keys[3], (D, HEADS * KH), D ** -0.5, 0.09375, ((0, 16),))
    sub_keys = draw_sub_keys(jax.random.fold_in(arg_keys[7], 71), 0)
    values = scatter_about(arg_keys[5], (SLAB_ROWS, D), 1.0, 6.0, ((0, 16),))
    cotangent = scatter_about(arg_keys[6], (TOKENS, D), 1.0, 6.0, ((0, 32),))
    return {"tokens": tokens, "owner": owner, "row_pick": row_pick, "query_weight": query_weight, "sub_keys": sub_keys, "values": values, "cotangent": cotangent}


def reference(tokens, owner, row_pick, query_weight, sub_keys, values, cotangent):
    query = jnp.dot(tokens, query_weight, preferred_element_type=jnp.float32).astype(jnp.bfloat16)
    query = query.reshape(TOKENS, HEADS, KH)
    full = jnp.einsum("thk,hrk->thr", query.astype(jnp.float32), sub_keys.astype(jnp.float32))
    score = jnp.take_along_axis(full, row_pick, axis=2) * (1.0 / (KH ** 0.5))
    top = jnp.max(score, axis=2, keepdims=True)
    expo = jnp.exp(score - top)
    weight = (expo / jnp.sum(expo, axis=2, keepdims=True)).astype(jnp.bfloat16)
    index = (owner[:, :, None] * VROWS_DEV + row_pick).astype(jnp.int32)
    blocks = TOKENS // TOK_DEV
    index_blocks = index.reshape(blocks, TOK_DEV, HEADS, TOPK)
    weight_blocks = weight.reshape(blocks, TOK_DEV, HEADS, TOPK)
    grad_blocks = cotangent.reshape(blocks, TOK_DEV, D)

    def read_block(pair):
        idx, wts = pair
        rows = values[idx].astype(jnp.float32)
        read = jnp.einsum("bhk,bhkd->bhd", wts.astype(jnp.float32), rows).astype(jnp.bfloat16)
        read = lax.optimization_barrier(read)
        return jnp.sum(read.astype(jnp.float32), axis=1).astype(jnp.bfloat16)

    memory_out = lax.map(read_block, (index_blocks, weight_blocks)).reshape(TOKENS, D)

    def add_block(total, trio):
        idx, wts, grd = trio
        terms = wts.astype(jnp.float32)[:, :, :, None] * grd.astype(jnp.float32)[:, None, None, :]
        return total.at[idx.reshape(-1)].add(terms.reshape(-1, D)), None

    start = jnp.zeros((SLAB_ROWS, D), jnp.float32)
    total, unused = lax.scan(add_block, start, (index_blocks, weight_blocks, grad_blocks))
    return memory_out, total.astype(jnp.bfloat16)
```

```python
import jax
import jax.numpy as jnp
from jax import lax
from jax.sharding import Mesh, PartitionSpec as P

INNER = 4


def body(tokens, owner, row_pick, query_weight, sub_keys, values, cotangent):
    tok_rows = tokens.shape[0]
    heads = owner.shape[1]
    width = tokens.shape[1]
    block_rows = values.shape[0]
    key_width = sub_keys.shape[2]
    far = lax.axis_size("far")
    near = lax.axis_size("near")
    copies = lax.axis_size("dp")
    groups = far * near
    layer = near * copies
    part = width // layer
    capacity = max(2, 3 * tok_rows * heads // (2 * groups))
    requests = tok_rows * heads
    f32, bf16 = jnp.float32, jnp.bfloat16
    y = lax.axis_index("dp")

    cot = cotangent.reshape(tok_rows, layer, part).transpose(1, 0, 2)
    cot = lax.all_to_all(cot, ("near", "dp"), split_axis=0, concat_axis=0, tiled=True)
    cot = lax.all_gather(cot, "far", axis=0, tiled=False)

    vals = values.reshape(block_rows, near, copies, part)
    vals = lax.dynamic_index_in_dim(vals, y, axis=2, keepdims=False).transpose(1, 0, 2)
    vals = lax.all_to_all(vals, "near", split_axis=0, concat_axis=0, tiled=True)

    own = query_weight.shape[0] // copies
    mine = lax.dynamic_slice_in_dim(query_weight, y * own, own, axis=0)
    qw = lax.all_gather(mine, ("far", "near", "dp"), axis=0, tiled=True)
    query = jnp.dot(tokens, qw, preferred_element_type=f32).astype(bf16)
    query = query.reshape(tok_rows, heads, key_width)
    full = jnp.einsum("thk,hrk->thr", query, sub_keys, preferred_element_type=f32)
    match = row_pick[:, :, :, None] == jnp.arange(block_rows, dtype=jnp.int32)[None, None, None, :]
    picked = jnp.sum(jnp.where(match, full[:, :, None, :], 0.0), axis=3)
    score = picked * (1.0 / key_width**0.5)
    top = jnp.max(score, axis=2, keepdims=True)
    expo = jnp.exp(score - top)
    weight = (expo / jnp.sum(expo, axis=2, keepdims=True)).astype(bf16)
    table = jnp.sum(jnp.where(match, weight.astype(f32)[:, :, :, None], 0.0), axis=2)
    table = table.astype(bf16).reshape(requests, block_rows)

    ids = jnp.arange(groups, dtype=jnp.int32)
    hits = owner[:, :, None] == ids[None, None, :]
    named = jnp.any(hits, axis=1)
    row = jnp.arange(tok_rows, dtype=jnp.int32)
    before = (row[:, None] > row[None, :]).astype(bf16)
    rank = jnp.dot(before, named.astype(bf16), preferred_element_type=f32).astype(jnp.int32)
    places = jnp.arange(capacity, dtype=jnp.int32)
    own_slot = hits & (rank[:, None, :] < capacity)
    slot = jnp.sum(jnp.where(own_slot, ids * capacity + rank[:, None, :], 0), axis=2).reshape(-1)
    dispatch = (
        jnp.arange(groups * capacity, dtype=jnp.int32)[:, None] == slot[None, :]
    ).astype(bf16)
    send = jnp.dot(dispatch, table, preferred_element_type=f32).astype(bf16)
    send = send.reshape(groups, capacity, block_rows)
    held = named[:, :, None] & (rank[:, :, None] == places)
    who = jnp.sum(jnp.where(held, row[:, None, None] + 1, 0), axis=0) - 1
    who = jnp.pad(who, ((0, 0), (0, block_rows - capacity)), constant_values=-1)
    send = jnp.concatenate([send, who.astype(bf16)[:, None, :]], axis=1)
    send = send.reshape(far, near, capacity + 1, block_rows)
    got = lax.all_to_all(send, "far", split_axis=0, concat_axis=0, tiled=True)
    got = lax.all_gather(got, ("near", "dp"), axis=0, tiled=False)
    got = got.transpose(1, 0, 2, 3, 4).reshape(far * layer, near, capacity + 1, block_rows)
    slots = got[:, :, :capacity, :]
    who = got[:, :, capacity, :capacity]
    pick = (who[:, None, :, :] == row.astype(bf16)[None, :, None, None]).astype(bf16)
    pick = pick.reshape(far * layer, tok_rows, near * capacity)
    cot = cot.reshape(far * layer, tok_rows, part)

    reads = jnp.einsum("dlcr,lrw->dlcw", slots, vals, preferred_element_type=f32).astype(bf16)
    reads = reads.reshape(far * layer, near * capacity, part)
    partial = jnp.einsum("dts,dsw->dtw", pick, reads, preferred_element_type=f32).astype(bf16)
    partial = partial.reshape(far, layer, tok_rows, part)
    total = lax.psum_scatter(partial, "far", scatter_dimension=0, tiled=False)
    total = lax.all_to_all(total, ("near", "dp"), split_axis=0, concat_axis=0, tiled=True)
    memory_out = total.transpose(1, 0, 2).reshape(tok_rows, width)

    terms = jnp.einsum("dts,dtw->dsw", pick, cot, preferred_element_type=f32).astype(bf16)
    terms = terms.reshape(far * layer, near, capacity, part)
    grad = jnp.einsum("dlcr,dlcw->lrw", slots, terms, preferred_element_type=f32).astype(bf16)
    grad = grad.reshape(layer, block_rows // copies, part)
    grad = lax.all_to_all(grad, ("near", "dp"), split_axis=0, concat_axis=0, tiled=True)
    grad_values = grad.transpose(1, 0, 2).reshape(block_rows // copies, width)
    return memory_out, grad_values


def solution(mesh):
    fsdp, dp = mesh.shape["fsdp"], mesh.shape["dp"]
    fine = Mesh(mesh.devices.reshape(fsdp // INNER, INNER, dp), ("far", "near", "dp"))
    rows, held = ("far", "near", "dp"), ("far", "near")
    placed = (
        P(rows, None),
        P(rows, None),
        P(rows, None, None),
        P(held, None),
        P(),
        P(held, None),
        P(rows, None),
    )
    return jax.shard_map(
        body,
        mesh=fine,
        in_specs=placed,
        out_specs=(P(rows, None), P(rows, None)),
        check_vma=False,
    )
```

```python
import functools
import jax
import jax.numpy as jnp
from jax import lax
from jax.experimental import pallas as pl
from jax.experimental.pallas import tpu as pltpu
from jax.sharding import Mesh, PartitionSpec as P

INNER = 4
MESH = pl.DeviceIdType.MESH
AXES = ("far", "high", "low", "dp")
ORDERS = (("far", "dp", "high", "low"), ("far", "high", "dp", "low"))


def place():
    near = lax.axis_index("near")
    return (lax.axis_index("far"), near // 2, near % 2, lax.axis_index("dp"))


def moved(me, sizes, off):
    return tuple(lax.rem(m + o, n) if o else m for m, o, n in zip(me, off, sizes))


def device(spot):
    return {"far": spot[0], "near": spot[1] * 2 + spot[2], "dp": spot[3]}


def tree(order, sizes):
    nodes = [((0, 0, 0, 0), -1, [])]
    for off, stage, copies in nodes:
        for k in range(stage + 1, len(order)):
            axis = AXES.index(order[k])
            for r in range(1, sizes[axis]):
                child = list(off)
                child[axis] = (child[axis] - r) % sizes[axis]
                copies.append((axis, r, len(nodes)))
                nodes.append((tuple(child), k, []))
    return nodes


def greet(peers):
    barrier = pltpu.get_barrier_semaphore()
    for spot in peers:
        pl.semaphore_signal(barrier, inc=1, device_id=device(spot), device_id_type=MESH)
    pl.semaphore_wait(barrier, len(peers))


def steps(sizes):
    found = []
    for axis, n in enumerate(sizes):
        for r in range(1, n):
            found.append(tuple(r if a == axis else 0 for a in range(4)))
    return found


def spread(me, sizes, plans, own, slot, started, send_sem, recv_sem):
    pending = {}
    longest = max(len(nodes) for nodes in plans)
    for number in range(longest):
        for item, nodes in enumerate(plans):
            if number >= len(nodes):
                continue
            off, stage, copies = nodes[number]
            if number:
                pending[item, number].wait_recv()
            here = moved(me, sizes, off)
            for axis, r, child in copies:
                step = tuple(r if a == axis else 0 for a in range(4))
                peer = moved(me, sizes, step)
                copy = pltpu.make_async_remote_copy(
                    src_ref=slot(item, here) if number else own(item, axis, peer),
                    dst_ref=slot(item, here),
                    send_sem=send_sem.at[item, child],
                    recv_sem=recv_sem.at[item, child],
                    device_id=device(peer),
                    device_id_type=MESH,
                )
                copy.start()
                pending[item, child] = copy
                started.append(copy)


def gather_kernel(sizes, qw_ref, val_ref, out_ref, vals_ref, send_sem, recv_sem, vsend, vrecv):
    me = place()
    half = qw_ref.shape[0] // 2
    part = vals_ref.shape[2]
    corner = (0, 1, 1, 0)
    greet([moved(me, sizes, s) for s in steps(sizes) + [corner]])
    for item in range(2):
        out_ref[me[0], me[1], me[2], me[3], item] = qw_ref[pl.ds(item * half, half), :]
    started = []

    def own(item, axis, peer):
        return qw_ref.at[pl.ds(item * half, half), :]

    def slot(item, spot):
        return out_ref.at[spot[0], spot[1], spot[2], spot[3], item]

    plans = [tree(order, sizes) for order in ORDERS]
    spread(me, sizes, plans, own, slot, started, send_sem, recv_sem)
    pushes = []
    for number, step in enumerate(((0, 1, 0, 0), (0, 0, 1, 0), corner)):
        peer = moved(me, sizes, step)
        first = ((peer[1] * 2 + peer[2]) * sizes[3] + peer[3]) * part
        copy = pltpu.make_async_remote_copy(
            src_ref=val_ref.at[:, pl.ds(pl.multiple_of(first, part), part)],
            dst_ref=vals_ref.at[me[1] * 2 + me[2]],
            send_sem=vsend.at[number],
            recv_sem=vrecv.at[number],
            device_id=device(peer),
            device_id_type=MESH,
        )
        copy.start()
        pushes.append(copy)
    first = ((me[1] * 2 + me[2]) * sizes[3] + me[3]) * part
    vals_ref[me[1] * 2 + me[2]] = val_ref[:, pl.ds(pl.multiple_of(first, part), part)]
    for copy in started:
        copy.wait_send()
    for copy in pushes:
        copy.wait()


def table_kernel(sizes, send_ref, out_ref, send_sem, recv_sem):
    me = place()
    half = send_ref.shape[2] // 2
    greet([moved(me, sizes, s) for s in steps(sizes)])
    out_ref[me[0], me[1], me[2], me[3]] = send_ref[me[0]]
    started = []

    def own(item, axis, peer):
        return send_ref.at[peer[0], :, pl.ds(item * half, half)]

    def slot(item, spot):
        return out_ref.at[spot[0], spot[1], spot[2], spot[3], :, pl.ds(item * half, half)]

    plans = [tree(order, sizes) for order in ORDERS]
    spread(me, sizes, plans, own, slot, started, send_sem, recv_sem)
    for copy in started:
        copy.wait_send()


VMEM = pl.BlockSpec(memory_space=pltpu.VMEM)


def gather(sizes, mine, values, near, part):
    count = sizes[0] * sizes[1] * sizes[2] * sizes[3]
    return pl.pallas_call(
        functools.partial(gather_kernel, sizes),
        out_shape=(
            jax.ShapeDtypeStruct(sizes + (2, mine.shape[0] // 2, mine.shape[1]), mine.dtype),
            jax.ShapeDtypeStruct((near, values.shape[0], part), values.dtype),
        ),
        in_specs=[VMEM] * 2,
        out_specs=(VMEM, VMEM),
        scratch_shapes=[
            pltpu.SemaphoreType.DMA((2, count)),
            pltpu.SemaphoreType.DMA((2, count)),
            pltpu.SemaphoreType.DMA((3,)),
            pltpu.SemaphoreType.DMA((3,)),
        ],
        compiler_params=pltpu.CompilerParams(collective_id=0, has_side_effects=True),
        name="gather_rows",
    )(mine, values)


def exchange(sizes, send):
    count = sizes[0] * sizes[1] * sizes[2] * sizes[3]
    return pl.pallas_call(
        functools.partial(table_kernel, sizes),
        out_shape=jax.ShapeDtypeStruct(sizes + send.shape[1:], send.dtype),
        in_specs=[VMEM],
        out_specs=VMEM,
        scratch_shapes=[
            pltpu.SemaphoreType.DMA((2, count)),
            pltpu.SemaphoreType.DMA((2, count)),
        ],
        compiler_params=pltpu.CompilerParams(collective_id=1, has_side_effects=True),
        name="exchange_tables",
    )(send)


def body(tokens, owner, row_pick, query_weight, sub_keys, values, cotangent):
    tok_rows = tokens.shape[0]
    heads = owner.shape[1]
    width = tokens.shape[1]
    block_rows = values.shape[0]
    key_width = sub_keys.shape[2]
    far = lax.axis_size("far")
    near = lax.axis_size("near")
    copies = lax.axis_size("dp")
    groups = far * near
    layer = near * copies
    part = width // layer
    capacity = max(2, 3 * tok_rows * heads // (2 * groups))
    requests = tok_rows * heads
    f32, bf16 = jnp.float32, jnp.bfloat16
    y = lax.axis_index("dp")

    cot = cotangent.reshape(tok_rows, layer, part).transpose(1, 0, 2)
    cot = lax.all_to_all(cot, ("near", "dp"), split_axis=0, concat_axis=0, tiled=True)
    cot = lax.all_gather(cot, "far", axis=0, tiled=False)

    own = query_weight.shape[0] // copies
    mine = lax.dynamic_slice_in_dim(query_weight, y * own, own, axis=0)
    sizes = (far, 2, near // 2, copies)
    qw, vals = gather(sizes, mine, values, near, part)
    qw = qw.reshape(width, -1)
    query = jnp.dot(tokens, qw, preferred_element_type=f32).astype(bf16)
    query = query.reshape(tok_rows, heads, key_width)
    full = jnp.einsum("thk,hrk->thr", query, sub_keys, preferred_element_type=f32)
    match = row_pick[:, :, :, None] == jnp.arange(block_rows, dtype=jnp.int32)[None, None, None, :]
    picked = jnp.sum(jnp.where(match, full[:, :, None, :], 0.0), axis=3)
    score = picked * (1.0 / key_width**0.5)
    top = jnp.max(score, axis=2, keepdims=True)
    expo = jnp.exp(score - top)
    weight = (expo / jnp.sum(expo, axis=2, keepdims=True)).astype(bf16)
    table = jnp.sum(jnp.where(match, weight.astype(f32)[:, :, :, None], 0.0), axis=2)
    table = table.astype(bf16).reshape(requests, block_rows)

    ids = jnp.arange(groups, dtype=jnp.int32)
    hits = owner[:, :, None] == ids[None, None, :]
    named = jnp.any(hits, axis=1)
    row = jnp.arange(tok_rows, dtype=jnp.int32)
    before = (row[:, None] > row[None, :]).astype(bf16)
    rank = jnp.dot(before, named.astype(bf16), preferred_element_type=f32).astype(jnp.int32)
    places = jnp.arange(capacity, dtype=jnp.int32)
    own_slot = hits & (rank[:, None, :] < capacity)
    slot = jnp.sum(jnp.where(own_slot, ids * capacity + rank[:, None, :], 0), axis=2).reshape(-1)
    dispatch = (
        jnp.arange(groups * capacity, dtype=jnp.int32)[:, None] == slot[None, :]
    ).astype(bf16)
    send = jnp.dot(dispatch, table, preferred_element_type=f32).astype(bf16)
    send = send.reshape(groups, capacity, block_rows)
    held = named[:, :, None] & (rank[:, :, None] == places)
    who = jnp.sum(jnp.where(held, row[:, None, None] + 1, 0), axis=0) - 1
    spare = 16 * -(-near // 16)
    who = who.astype(bf16).reshape(far, near, capacity)
    who = jnp.pad(who, ((0, 0), (0, spare - near), (0, block_rows - capacity)))
    send = jnp.concatenate([send.reshape(far, near * capacity, block_rows), who], axis=1)
    got = exchange(sizes, send).reshape(far * layer, near * capacity + spare, block_rows)
    slots = got[:, : near * capacity].reshape(far * layer, near, capacity, block_rows)
    who = got[:, near * capacity : near * capacity + near, :capacity]
    pick = (who[:, None, :, :] == row.astype(bf16)[None, :, None, None]).astype(bf16)
    pick = pick.reshape(far * layer, tok_rows, near * capacity)
    cot = cot.reshape(far * layer, tok_rows, part)

    reads = jnp.einsum("dlcr,lrw->dlcw", slots, vals, preferred_element_type=f32).astype(bf16)
    reads = reads.reshape(far * layer, near * capacity, part)
    partial = jnp.einsum("dts,dsw->dtw", pick, reads, preferred_element_type=f32).astype(bf16)
    partial = partial.reshape(far, layer, tok_rows, part)
    total = lax.psum_scatter(partial, "far", scatter_dimension=0, tiled=False)
    total = lax.all_to_all(total, ("near", "dp"), split_axis=0, concat_axis=0, tiled=True)
    memory_out = total.transpose(1, 0, 2).reshape(tok_rows, width)

    terms = jnp.einsum("dts,dtw->dsw", pick, cot, preferred_element_type=f32).astype(bf16)
    terms = terms.reshape(far * layer, near, capacity, part)
    grad = jnp.einsum("dlcr,dlcw->lrw", slots, terms, preferred_element_type=f32).astype(bf16)
    grad = grad.reshape(layer, block_rows // copies, part)
    grad = lax.all_to_all(grad, ("near", "dp"), split_axis=0, concat_axis=0, tiled=True)
    grad_values = grad.transpose(1, 0, 2).reshape(block_rows // copies, width)
    return memory_out, grad_values


def solution(mesh):
    fsdp, dp = mesh.shape["fsdp"], mesh.shape["dp"]
    fine = Mesh(mesh.devices.reshape(fsdp // INNER, INNER, dp), ("far", "near", "dp"))
    rows, held = ("far", "near", "dp"), ("far", "near")
    placed = (
        P(rows, None),
        P(rows, None),
        P(rows, None, None),
        P(held, None),
        P(),
        P(held, None),
        P(rows, None),
    )
    return jax.shard_map(
        body,
        mesh=fine,
        in_specs=placed,
        out_specs=(P(rows, None), P(rows, None)),
        check_vma=False,
    )
```

```python
import functools
import jax
import jax.numpy as jnp
from jax import lax
from jax.experimental import pallas as pl
from jax.experimental.pallas import tpu as pltpu
from jax.sharding import Mesh, PartitionSpec as P

INNER = 4
MESH = pl.DeviceIdType.MESH
AXES = ("far", "high", "low", "dp")
ORDERS = (("far", "dp", "high", "low"), ("far", "high", "dp", "low"))


def place():
    near = lax.axis_index("near")
    return (lax.axis_index("far"), near // 2, near % 2, lax.axis_index("dp"))


def moved(me, sizes, off):
    return tuple(lax.rem(m + o, n) if o else m for m, o, n in zip(me, off, sizes))


def device(spot):
    return {"far": spot[0], "near": spot[1] * 2 + spot[2], "dp": spot[3]}


def tree(order, sizes):
    nodes = [((0, 0, 0, 0), -1, [])]
    for off, stage, copies in nodes:
        for k in range(stage + 1, len(order)):
            axis = AXES.index(order[k])
            for r in range(1, sizes[axis]):
                child = list(off)
                child[axis] = (child[axis] - r) % sizes[axis]
                copies.append((axis, r, len(nodes)))
                nodes.append((tuple(child), k, []))
    return nodes


def greet(peers):
    barrier = pltpu.get_barrier_semaphore()
    for spot in peers:
        pl.semaphore_signal(barrier, inc=1, device_id=device(spot), device_id_type=MESH)
    pl.semaphore_wait(barrier, len(peers))


def steps(sizes):
    found = []
    for axis, n in enumerate(sizes):
        for r in range(1, n):
            found.append(tuple(r if a == axis else 0 for a in range(4)))
    return found


def spread(me, sizes, plans, own, slot, started, send_sem, recv_sem, events=()):
    pending = {}
    longest = max(len(nodes) for nodes in plans)
    for number in range(longest):
        for when, event in events:
            if when == number:
                event()
        for item, nodes in enumerate(plans):
            if number >= len(nodes):
                continue
            off, stage, copies = nodes[number]
            if number:
                pending[item, number].wait_recv()
            here = moved(me, sizes, off)
            for axis, r, child in copies:
                step = tuple(r if a == axis else 0 for a in range(4))
                peer = moved(me, sizes, step)
                copy = pltpu.make_async_remote_copy(
                    src_ref=slot(item, here) if number else own(item, axis, peer),
                    dst_ref=slot(item, here),
                    send_sem=send_sem.at[item, child],
                    recv_sem=recv_sem.at[item, child],
                    device_id=device(peer),
                    device_id_type=MESH,
                )
                copy.start()
                pending[item, child] = copy
                started.append(copy)


def rank_in_layer(spot, sizes):
    return (spot[1] * 2 + spot[2]) * sizes[3] + spot[3]


def layer_peers(me, sizes):
    layer = sizes[1] * sizes[2] * sizes[3]
    mine = rank_in_layer(me, sizes)
    for r in range(1, layer):
        j = lax.rem(mine + r, layer)
        near = j // sizes[3]
        yield r - 1, j, (me[0], near // 2, near % 2, lax.rem(j, sizes[3]))


def columns(j, part):
    return pl.ds(pl.multiple_of(j * part, part), part)


def gather_kernel(
    sizes, qw_ref, val_ref, cot_ref, out_ref, vals_ref, hop_ref,
    send_sem, recv_sem, vsend, vrecv, csend, crecv, hsend, hrecv, local,
):
    me = place()
    far = sizes[0]
    z = me[0]
    mine = rank_in_layer(me, sizes)
    width = hop_ref.shape[3]
    half = qw_ref.shape[0] // 2
    part = vals_ref.shape[2]
    corner = (0, 1, 1, 0)
    beside = [moved(me, sizes, s) for s in steps((far, 1, 1, 1))]
    greet(beside + [spot for _, _, spot in layer_peers(me, sizes)])
    for item in range(2):
        out_ref[me[0], me[1], me[2], me[3], item] = qw_ref[pl.ds(item * half, half), :]
    started = []

    def own(item, axis, peer):
        return qw_ref.at[pl.ds(item * half, half), :]

    def slot(item, spot):
        return out_ref.at[spot[0], spot[1], spot[2], spot[3], item]

    cuts = []

    def hop(side):
        return pltpu.make_async_remote_copy(
            src_ref=hop_ref.at[0],
            dst_ref=hop_ref.at[1 + side],
            send_sem=hsend.at[side],
            recv_sem=hrecv.at[side],
            device_id=device((z + 1 - 2 * side,) + me[1:]),
            device_id_type=MESH,
        )

    def cut():
        for number, j, spot in layer_peers(me, sizes):
            copy = pltpu.make_async_remote_copy(
                src_ref=cot_ref.at[:, columns(j, width)],
                dst_ref=hop_ref.at[0, mine],
                send_sem=csend.at[number],
                recv_sem=crecv.at[number],
                device_id=device(spot),
                device_id_type=MESH,
            )
            copy.start()
            cuts.append(copy)
        keep = pltpu.make_async_copy(
            cot_ref.at[:, columns(mine, width)], hop_ref.at[0, mine], local
        )
        keep.start()
        cuts.append(keep)

    def forward():
        for copy in cuts[:-1]:
            copy.wait_recv()
        cuts[-1].wait()
        pl.when(z < far - 1)(lambda: hop(0).start())
        pl.when(z > 0)(lambda: hop(1).start())

    plans = [tree(order, sizes) for order in ORDERS]
    events = ((1, cut), (12, forward))
    spread(me, sizes, plans, own, slot, started, send_sem, recv_sem, events)
    started.extend(cuts[:-1])
    pushes = []
    for number, step in enumerate(((0, 1, 0, 0), (0, 0, 1, 0), corner)):
        peer = moved(me, sizes, step)
        first = ((peer[1] * 2 + peer[2]) * sizes[3] + peer[3]) * part
        copy = pltpu.make_async_remote_copy(
            src_ref=val_ref.at[:, pl.ds(pl.multiple_of(first, part), part)],
            dst_ref=vals_ref.at[me[1] * 2 + me[2]],
            send_sem=vsend.at[number],
            recv_sem=vrecv.at[number],
            device_id=device(peer),
            device_id_type=MESH,
        )
        copy.start()
        pushes.append(copy)
    first = ((me[1] * 2 + me[2]) * sizes[3] + me[3]) * part
    vals_ref[me[1] * 2 + me[2]] = val_ref[:, pl.ds(pl.multiple_of(first, part), part)]
    for copy in started:
        copy.wait_send()
    for copy in pushes:
        copy.wait()
    pl.when(z < far - 1)(lambda: hop(0).wait_send())
    pl.when(z > 0)(lambda: hop(0).wait_recv())
    pl.when(z > 0)(lambda: hop(1).wait_send())
    pl.when(z < far - 1)(lambda: hop(1).wait_recv())


def push_layer(me, sizes, source, target, send_sem, recv_sem):
    mine = rank_in_layer(me, sizes)
    part = source.shape[2]
    copies = []
    for number, j, spot in layer_peers(me, sizes):
        copy = pltpu.make_async_remote_copy(
            src_ref=source.at[j],
            dst_ref=target.at[:, columns(mine, part)],
            send_sem=send_sem.at[number],
            recv_sem=recv_sem.at[number],
            device_id=device(spot),
            device_id_type=MESH,
        )
        copy.start()
        copies.append(copy)
    target[:, columns(mine, part)] = source[mine]
    for copy in copies:
        copy.wait()


def push_kernel(sizes, grad_ref, out_ref, send_sem, recv_sem):
    me = place()
    greet([spot for _, _, spot in layer_peers(me, sizes)])
    push_layer(me, sizes, grad_ref, out_ref, send_sem, recv_sem)


def line_kernel(
    sizes, part_ref, hop_ref, out_ref, cot_ref, sums, total,
    ssend, srecv, hsend, hrecv, csend, crecv, local,
):
    me = place()
    far = sizes[0]
    z = me[0]
    beside = [moved(me, sizes, s) for s in steps((far, 1, 1, 1))]
    greet(beside + [spot for _, _, spot in layer_peers(me, sizes)])
    near = ((0, z), (1, z - 1), (2, z + 1))
    inside = (z >= 0, z > 0, z < far - 1)

    def keep(k):
        return pltpu.make_async_copy(hop_ref.at[k], cot_ref.at[near[k][1]], local.at[k])

    for k in range(3):
        pl.when(inside[k])(lambda k=k: keep(k).start())

    def where(side):
        return z if side == 0 else far - 1 - z

    def toward(side):
        return device((z + 1 - 2 * side,) + me[1:])

    def goal(side, s):
        return far - 1 - s + z if side == 0 else s - far + 1 + z

    def summed(side, s, first):
        d = goal(side, s)
        return pltpu.make_async_remote_copy(
            src_ref=part_ref.at[d] if first else sums.at[side, d],
            dst_ref=sums.at[side, d],
            send_sem=ssend.at[side, s],
            recv_sem=srecv.at[side, s],
            device_id=toward(side),
            device_id_type=MESH,
        )

    def arrived(side, s):
        d = goal(side, s + 1)
        return pltpu.make_async_remote_copy(
            src_ref=sums.at[side, d],
            dst_ref=sums.at[side, d],
            send_sem=ssend.at[side, s],
            recv_sem=srecv.at[side, s],
            device_id=toward(side),
            device_id_type=MESH,
        )

    def passed(side, h):
        c = z - (h - 1) if side == 0 else z + (h - 1)
        return pltpu.make_async_remote_copy(
            src_ref=hop_ref.at[1 + side] if h == 2 else cot_ref.at[c],
            dst_ref=cot_ref.at[c],
            send_sem=hsend.at[side, h],
            recv_sem=hrecv.at[side, h],
            device_id=toward(side),
            device_id_type=MESH,
        )

    def came(side, h):
        c = z - h if side == 0 else z + h
        return pltpu.make_async_remote_copy(
            src_ref=cot_ref.at[c],
            dst_ref=cot_ref.at[c],
            send_sem=hsend.at[side, h],
            recv_sem=hrecv.at[side, h],
            device_id=toward(side),
            device_id_type=MESH,
        )

    def add(side, s):
        d = goal(side, s)

        @pl.loop(0, sums.shape[2])
        def _(j):
            here = sums[side, d, j].astype(jnp.float32) + part_ref[d, j].astype(jnp.float32)
            sums[side, d, j] = here.astype(sums.dtype)

    for s in range(far - 1):
        for side in range(2):
            pl.when(where(side) == 0)(lambda: summed(side, s, True).start())
            if s:

                @pl.when((where(side) > 0) & (where(side) <= s))
                def _():
                    arrived(side, s - 1).wait_recv()
                    add(side, s)
                    summed(side, s, False).start()

        h = s + 2
        if h < far:
            for side in range(2):
                if h > 2:
                    pl.when(where(side) >= h - 1)(lambda: came(side, h - 1).wait_recv())
                active = (where(side) >= h - 1) & (where(side) < far - 1)
                pl.when(active)(lambda: passed(side, h).start())

    for side in range(2):
        pl.when(where(side) > 0)(lambda: arrived(side, far - 2).wait_recv())

    @pl.loop(0, total.shape[0])
    def _(j):
        here = part_ref[z, j].astype(jnp.float32)
        up = jnp.where(z > 0, sums[0, z, j].astype(jnp.float32), 0.0)
        down = jnp.where(z < far - 1, sums[1, z, j].astype(jnp.float32), 0.0)
        total[j] = (here + up + down).astype(total.dtype)

    push_layer(me, sizes, total, out_ref, csend, crecv)
    for side in range(2):
        for s in range(far - 1):
            pl.when(where(side) == 0)(lambda: summed(side, s, True).wait_send())
            if s:
                busy = (where(side) > 0) & (where(side) <= s)
                pl.when(busy)(lambda: summed(side, s, False).wait_send())
        for h in range(2, far):
            active = (where(side) >= h - 1) & (where(side) < far - 1)
            pl.when(active)(lambda: passed(side, h).wait_send())
        if far > 2:
            pl.when(where(side) >= far - 1)(lambda: came(side, far - 1).wait_recv())
    for k in range(3):
        pl.when(inside[k])(lambda k=k: keep(k).wait())


def table_kernel(sizes, send_ref, out_ref, send_sem, recv_sem):
    me = place()
    half = send_ref.shape[2] // 2
    greet([moved(me, sizes, s) for s in steps(sizes)])
    out_ref[me[0], me[1], me[2], me[3]] = send_ref[me[0]]
    started = []

    def own(item, axis, peer):
        return send_ref.at[peer[0], :, pl.ds(item * half, half)]

    def slot(item, spot):
        return out_ref.at[spot[0], spot[1], spot[2], spot[3], :, pl.ds(item * half, half)]

    plans = [tree(order, sizes) for order in ORDERS]
    spread(me, sizes, plans, own, slot, started, send_sem, recv_sem)
    for copy in started:
        copy.wait_send()


VMEM = pl.BlockSpec(memory_space=pltpu.VMEM)


def gather(sizes, mine, values, cotangent, near, part):
    layer = near * sizes[3]
    count = sizes[0] * sizes[1] * sizes[2] * sizes[3]
    return pl.pallas_call(
        functools.partial(gather_kernel, sizes),
        out_shape=(
            jax.ShapeDtypeStruct(sizes + (2, mine.shape[0] // 2, mine.shape[1]), mine.dtype),
            jax.ShapeDtypeStruct((near, values.shape[0], part), values.dtype),
            jax.ShapeDtypeStruct((3, layer, cotangent.shape[0], part), cotangent.dtype),
        ),
        in_specs=[VMEM] * 3,
        out_specs=(VMEM, VMEM, VMEM),
        scratch_shapes=[
            pltpu.SemaphoreType.DMA((2, count)),
            pltpu.SemaphoreType.DMA((2, count)),
            pltpu.SemaphoreType.DMA((3,)),
            pltpu.SemaphoreType.DMA((3,)),
            pltpu.SemaphoreType.DMA((layer,)),
            pltpu.SemaphoreType.DMA((layer,)),
            pltpu.SemaphoreType.DMA((2,)),
            pltpu.SemaphoreType.DMA((2,)),
            pltpu.SemaphoreType.DMA,
        ],
        compiler_params=pltpu.CompilerParams(collective_id=0, has_side_effects=True),
        name="gather_rows",
    )(mine, values, cotangent)


def push(sizes, grad):
    layer, rows, part = grad.shape
    return pl.pallas_call(
        functools.partial(push_kernel, sizes),
        out_shape=jax.ShapeDtypeStruct((rows, layer * part), grad.dtype),
        in_specs=[VMEM],
        out_specs=VMEM,
        scratch_shapes=[pltpu.SemaphoreType.DMA((layer,)), pltpu.SemaphoreType.DMA((layer,))],
        compiler_params=pltpu.CompilerParams(collective_id=2, has_side_effects=True),
        name="push_gradient",
    )(grad)


def line(sizes, partial, hops):
    far, layer, rows, part = partial.shape
    return pl.pallas_call(
        functools.partial(line_kernel, sizes),
        out_shape=(
            jax.ShapeDtypeStruct((rows, layer * part), partial.dtype),
            jax.ShapeDtypeStruct((far,) + hops.shape[1:], hops.dtype),
        ),
        in_specs=[VMEM] * 2,
        out_specs=(VMEM, VMEM),
        scratch_shapes=[
            pltpu.VMEM((2,) + partial.shape, partial.dtype),
            pltpu.VMEM(partial.shape[1:], partial.dtype),
            pltpu.SemaphoreType.DMA((2, far)),
            pltpu.SemaphoreType.DMA((2, far)),
            pltpu.SemaphoreType.DMA((2, far)),
            pltpu.SemaphoreType.DMA((2, far)),
            pltpu.SemaphoreType.DMA((layer,)),
            pltpu.SemaphoreType.DMA((layer,)),
            pltpu.SemaphoreType.DMA((3,)),
        ],
        compiler_params=pltpu.CompilerParams(collective_id=3, has_side_effects=True),
        name="sum_line",
    )(partial, hops)


def exchange(sizes, send):
    count = sizes[0] * sizes[1] * sizes[2] * sizes[3]
    return pl.pallas_call(
        functools.partial(table_kernel, sizes),
        out_shape=jax.ShapeDtypeStruct(sizes + send.shape[1:], send.dtype),
        in_specs=[VMEM],
        out_specs=VMEM,
        scratch_shapes=[
            pltpu.SemaphoreType.DMA((2, count)),
            pltpu.SemaphoreType.DMA((2, count)),
        ],
        compiler_params=pltpu.CompilerParams(collective_id=1, has_side_effects=True),
        name="exchange_tables",
    )(send)


def body(tokens, owner, row_pick, query_weight, sub_keys, values, cotangent):
    tok_rows = tokens.shape[0]
    heads = owner.shape[1]
    width = tokens.shape[1]
    block_rows = values.shape[0]
    key_width = sub_keys.shape[2]
    far = lax.axis_size("far")
    near = lax.axis_size("near")
    copies = lax.axis_size("dp")
    groups = far * near
    layer = near * copies
    part = width // layer
    capacity = max(2, 3 * tok_rows * heads // (2 * groups))
    requests = tok_rows * heads
    f32, bf16 = jnp.float32, jnp.bfloat16
    y = lax.axis_index("dp")

    own = query_weight.shape[0] // copies
    mine = lax.dynamic_slice_in_dim(query_weight, y * own, own, axis=0)
    sizes = (far, 2, near // 2, copies)
    qw, vals, hops = gather(sizes, mine, values, cotangent, near, part)
    qw = qw.reshape(width, -1)
    query = jnp.dot(tokens, qw, preferred_element_type=f32).astype(bf16)
    query = query.reshape(tok_rows, heads, key_width)
    full = jnp.einsum("thk,hrk->thr", query, sub_keys, preferred_element_type=f32)
    match = row_pick[:, :, :, None] == jnp.arange(block_rows, dtype=jnp.int32)[None, None, None, :]
    picked = jnp.sum(jnp.where(match, full[:, :, None, :], 0.0), axis=3)
    score = picked * (1.0 / key_width**0.5)
    top = jnp.max(score, axis=2, keepdims=True)
    expo = jnp.exp(score - top)
    weight = (expo / jnp.sum(expo, axis=2, keepdims=True)).astype(bf16)
    table = jnp.sum(jnp.where(match, weight.astype(f32)[:, :, :, None], 0.0), axis=2)
    table = table.astype(bf16).reshape(requests, block_rows)

    ids = jnp.arange(groups, dtype=jnp.int32)
    hits = owner[:, :, None] == ids[None, None, :]
    named = jnp.any(hits, axis=1)
    row = jnp.arange(tok_rows, dtype=jnp.int32)
    before = (row[:, None] > row[None, :]).astype(bf16)
    rank = jnp.dot(before, named.astype(bf16), preferred_element_type=f32).astype(jnp.int32)
    places = jnp.arange(capacity, dtype=jnp.int32)
    own_slot = hits & (rank[:, None, :] < capacity)
    slot = jnp.sum(jnp.where(own_slot, ids * capacity + rank[:, None, :], 0), axis=2).reshape(-1)
    dispatch = (
        jnp.arange(groups * capacity, dtype=jnp.int32)[:, None] == slot[None, :]
    ).astype(bf16)
    send = jnp.dot(dispatch, table, preferred_element_type=f32).astype(bf16)
    send = send.reshape(groups, capacity, block_rows)
    held = named[:, :, None] & (rank[:, :, None] == places)
    who = jnp.sum(jnp.where(held, row[:, None, None] + 1, 0), axis=0) - 1
    spare = 16 * -(-near // 16)
    who = who.astype(bf16).reshape(far, near, capacity)
    who = jnp.pad(who, ((0, 0), (0, spare - near), (0, block_rows - capacity)))
    send = jnp.concatenate([send.reshape(far, near * capacity, block_rows), who], axis=1)
    got = exchange(sizes, send).reshape(far * layer, near * capacity + spare, block_rows)
    slots = got[:, : near * capacity].reshape(far * layer, near, capacity, block_rows)
    who = got[:, near * capacity : near * capacity + near, :capacity]
    pick = (who[:, None, :, :] == row.astype(bf16)[None, :, None, None]).astype(bf16)
    pick = pick.reshape(far * layer, tok_rows, near * capacity)

    reads = jnp.einsum("dlcr,lrw->dlcw", slots, vals, preferred_element_type=f32).astype(bf16)
    reads = reads.reshape(far * layer, near * capacity, part)
    partial = jnp.einsum("dts,dsw->dtw", pick, reads, preferred_element_type=f32).astype(bf16)
    partial = partial.reshape(far, layer, tok_rows, part)
    memory_out, cot = line(sizes, partial, hops)
    cot = cot.reshape(far * layer, tok_rows, part)

    terms = jnp.einsum("dts,dtw->dsw", pick, cot, preferred_element_type=f32).astype(bf16)
    terms = terms.reshape(far * layer, near, capacity, part)
    grad = jnp.einsum("dlcr,dlcw->lrw", slots, terms, preferred_element_type=f32).astype(bf16)
    grad = grad.reshape(layer, block_rows // copies, part)
    grad_values = push(sizes, grad)
    return memory_out, grad_values


def solution(mesh):
    fsdp, dp = mesh.shape["fsdp"], mesh.shape["dp"]
    fine = Mesh(mesh.devices.reshape(fsdp // INNER, INNER, dp), ("far", "near", "dp"))
    rows, held = ("far", "near", "dp"), ("far", "near")
    placed = (
        P(rows, None),
        P(rows, None),
        P(rows, None, None),
        P(held, None),
        P(),
        P(held, None),
        P(rows, None),
    )
    return jax.shard_map(
        body,
        mesh=fine,
        in_specs=placed,
        out_specs=(P(rows, None), P(rows, None)),
        check_vma=False,
    )
```

```python
import functools
import jax
import jax.numpy as jnp
from jax import lax
from jax.experimental import pallas as pl
from jax.experimental.pallas import tpu as pltpu
from jax.sharding import Mesh, PartitionSpec as P

INNER = 4
CHUNKS = 4
MESH = pl.DeviceIdType.MESH
AXES = ("far", "high", "low", "dp")
ORDERS = (("far", "dp", "high", "low"), ("far", "high", "dp", "low"))


def place():
    near = lax.axis_index("near")
    return (lax.axis_index("far"), near // 2, near % 2, lax.axis_index("dp"))


def moved(me, sizes, off):
    return tuple(lax.rem(m + o, n) if o else m for m, o, n in zip(me, off, sizes))


def device(spot):
    return {"far": spot[0], "near": spot[1] * 2 + spot[2], "dp": spot[3]}


def tree(order, sizes):
    nodes = [((0, 0, 0, 0), -1, [])]
    for off, stage, copies in nodes:
        for k in range(stage + 1, len(order)):
            axis = AXES.index(order[k])
            for r in range(1, sizes[axis]):
                child = list(off)
                child[axis] = (child[axis] - r) % sizes[axis]
                copies.append((axis, r, len(nodes)))
                nodes.append((tuple(child), k, []))
    return nodes


def greet(peers):
    barrier = pltpu.get_barrier_semaphore()
    for spot in peers:
        pl.semaphore_signal(barrier, inc=1, device_id=device(spot), device_id_type=MESH)
    pl.semaphore_wait(barrier, len(peers))


def steps(sizes):
    found = []
    for axis, n in enumerate(sizes):
        for r in range(1, n):
            found.append(tuple(r if a == axis else 0 for a in range(4)))
    return found


def spread(me, sizes, plans, own, slot, started, send_sem, recv_sem, events=()):
    pending = {}
    longest = max(len(nodes) for nodes in plans)
    for number in range(longest):
        for when, event in events:
            if when == number:
                event()
        for item, nodes in enumerate(plans):
            if number >= len(nodes):
                continue
            off, stage, copies = nodes[number]
            if number:
                pending[item, number].wait_recv()
            here = moved(me, sizes, off)
            for axis, r, child in copies:
                step = tuple(r if a == axis else 0 for a in range(4))
                peer = moved(me, sizes, step)
                copy = pltpu.make_async_remote_copy(
                    src_ref=slot(item, here) if number else own(item, axis, peer),
                    dst_ref=slot(item, here),
                    send_sem=send_sem.at[item, child],
                    recv_sem=recv_sem.at[item, child],
                    device_id=device(peer),
                    device_id_type=MESH,
                )
                copy.start()
                pending[item, child] = copy
                started.append(copy)


def rank_in_layer(spot, sizes):
    return (spot[1] * 2 + spot[2]) * sizes[3] + spot[3]


def layer_peers(me, sizes):
    layer = sizes[1] * sizes[2] * sizes[3]
    mine = rank_in_layer(me, sizes)
    for r in range(1, layer):
        j = lax.rem(mine + r, layer)
        near = j // sizes[3]
        yield r - 1, j, (me[0], near // 2, near % 2, lax.rem(j, sizes[3]))


def columns(j, part):
    return pl.ds(pl.multiple_of(j * part, part), part)


def gather_kernel(
    sizes, qw_ref, val_ref, cot_ref, out_ref, vals_ref, hop_ref,
    send_sem, recv_sem, vsend, vrecv, csend, crecv, hsend, hrecv, local,
):
    me = place()
    far = sizes[0]
    z = me[0]
    mine = rank_in_layer(me, sizes)
    width = hop_ref.shape[3]
    half = qw_ref.shape[0] // 2
    part = vals_ref.shape[2]
    corner = (0, 1, 1, 0)
    beside = [moved(me, sizes, s) for s in steps((far, 1, 1, 1))]
    greet(beside + [spot for _, _, spot in layer_peers(me, sizes)])
    for item in range(2):
        out_ref[me[0], me[1], me[2], me[3], item] = qw_ref[pl.ds(item * half, half), :]
    started = []

    def own(item, axis, peer):
        return qw_ref.at[pl.ds(item * half, half), :]

    def slot(item, spot):
        return out_ref.at[spot[0], spot[1], spot[2], spot[3], item]

    cuts = []

    def hop(side):
        return pltpu.make_async_remote_copy(
            src_ref=hop_ref.at[0],
            dst_ref=hop_ref.at[1 + side],
            send_sem=hsend.at[side],
            recv_sem=hrecv.at[side],
            device_id=device((z + 1 - 2 * side,) + me[1:]),
            device_id_type=MESH,
        )

    def cut():
        for number, j, spot in layer_peers(me, sizes):
            copy = pltpu.make_async_remote_copy(
                src_ref=cot_ref.at[:, columns(j, width)],
                dst_ref=hop_ref.at[0, mine],
                send_sem=csend.at[number],
                recv_sem=crecv.at[number],
                device_id=device(spot),
                device_id_type=MESH,
            )
            copy.start()
            cuts.append(copy)
        keep = pltpu.make_async_copy(
            cot_ref.at[:, columns(mine, width)], hop_ref.at[0, mine], local
        )
        keep.start()
        cuts.append(keep)

    def forward():
        for copy in cuts[:-1]:
            copy.wait_recv()
        cuts[-1].wait()
        pl.when(z < far - 1)(lambda: hop(0).start())
        pl.when(z > 0)(lambda: hop(1).start())

    plans = [tree(order, sizes) for order in ORDERS]
    events = ((1, cut), (12, forward))
    spread(me, sizes, plans, own, slot, started, send_sem, recv_sem, events)
    started.extend(cuts[:-1])
    pushes = []
    for number, step in enumerate(((0, 1, 0, 0), (0, 0, 1, 0), corner)):
        peer = moved(me, sizes, step)
        first = ((peer[1] * 2 + peer[2]) * sizes[3] + peer[3]) * part
        copy = pltpu.make_async_remote_copy(
            src_ref=val_ref.at[:, pl.ds(pl.multiple_of(first, part), part)],
            dst_ref=vals_ref.at[me[1] * 2 + me[2]],
            send_sem=vsend.at[number],
            recv_sem=vrecv.at[number],
            device_id=device(peer),
            device_id_type=MESH,
        )
        copy.start()
        pushes.append(copy)
    first = ((me[1] * 2 + me[2]) * sizes[3] + me[3]) * part
    vals_ref[me[1] * 2 + me[2]] = val_ref[:, pl.ds(pl.multiple_of(first, part), part)]
    for copy in started:
        copy.wait_send()
    for copy in pushes:
        copy.wait()
    pl.when(z < far - 1)(lambda: hop(0).wait_send())
    pl.when(z > 0)(lambda: hop(0).wait_recv())
    pl.when(z > 0)(lambda: hop(1).wait_send())
    pl.when(z < far - 1)(lambda: hop(1).wait_recv())


def push_layer(me, sizes, source, target, send_sem, recv_sem):
    mine = rank_in_layer(me, sizes)
    part = source.shape[2]
    copies = []
    for number, j, spot in layer_peers(me, sizes):
        copy = pltpu.make_async_remote_copy(
            src_ref=source.at[j],
            dst_ref=target.at[:, columns(mine, part)],
            send_sem=send_sem.at[number],
            recv_sem=recv_sem.at[number],
            device_id=device(spot),
            device_id_type=MESH,
        )
        copy.start()
        copies.append(copy)
    target[:, columns(mine, part)] = source[mine]
    for copy in copies:
        copy.wait()


def push_kernel(sizes, grad_ref, out_ref, send_sem, recv_sem):
    me = place()
    greet([spot for _, _, spot in layer_peers(me, sizes)])
    push_layer(me, sizes, grad_ref, out_ref, send_sem, recv_sem)


def line_kernel(
    sizes, part_ref, hop_ref, out_ref, cot_ref, sums, total,
    ssend, srecv, hsend, hrecv, csend, crecv, local,
):
    me = place()
    far = sizes[0]
    z = me[0]
    beside = [moved(me, sizes, s) for s in steps((far, 1, 1, 1))]
    greet(beside + [spot for _, _, spot in layer_peers(me, sizes)])
    near = ((0, z), (1, z - 1), (2, z + 1))
    inside = (z >= 0, z > 0, z < far - 1)

    def keep(k):
        return pltpu.make_async_copy(hop_ref.at[k], cot_ref.at[near[k][1]], local.at[k])

    for k in range(3):
        pl.when(inside[k])(lambda k=k: keep(k).start())

    chunks = ssend.shape[2]
    size = total.shape[0] // chunks
    mine = rank_in_layer(me, sizes)
    part = total.shape[2]

    def chunk(q):
        return pl.ds(q * size, size)

    def give(j):
        near, y = j // sizes[3], j % sizes[3]
        return pltpu.make_async_remote_copy(
            src_ref=total.at[j],
            dst_ref=out_ref.at[:, columns(mine, part)],
            send_sem=csend.at[j],
            recv_sem=crecv.at[mine],
            device_id=device((z, near // 2, near % 2, y)),
            device_id_type=MESH,
        )

    def given(j):
        return pltpu.make_async_remote_copy(
            src_ref=total.at[j],
            dst_ref=out_ref.at[:, columns(j, part)],
            send_sem=csend.at[j],
            recv_sem=crecv.at[j],
            device_id=device((z, (j // sizes[3]) // 2, (j // sizes[3]) % 2, j % sizes[3])),
            device_id_type=MESH,
        )

    def where(side):
        return z if side == 0 else far - 1 - z

    def toward(side):
        return device((z + 1 - 2 * side,) + me[1:])

    def goal(side, s):
        return far - 1 - s + z if side == 0 else s - far + 1 + z

    def summed(side, s, first, q):
        d = goal(side, s)
        return pltpu.make_async_remote_copy(
            src_ref=part_ref.at[d, chunk(q)] if first else sums.at[side, d, chunk(q)],
            dst_ref=sums.at[side, d, chunk(q)],
            send_sem=ssend.at[side, s, q],
            recv_sem=srecv.at[side, s, q],
            device_id=toward(side),
            device_id_type=MESH,
        )

    def arrived(side, s, q):
        d = goal(side, s + 1)
        return pltpu.make_async_remote_copy(
            src_ref=sums.at[side, d, chunk(q)],
            dst_ref=sums.at[side, d, chunk(q)],
            send_sem=ssend.at[side, s, q],
            recv_sem=srecv.at[side, s, q],
            device_id=toward(side),
            device_id_type=MESH,
        )

    def passed(side, h):
        c = z - (h - 1) if side == 0 else z + (h - 1)
        return pltpu.make_async_remote_copy(
            src_ref=hop_ref.at[1 + side] if h == 2 else cot_ref.at[c],
            dst_ref=cot_ref.at[c],
            send_sem=hsend.at[side, h],
            recv_sem=hrecv.at[side, h],
            device_id=toward(side),
            device_id_type=MESH,
        )

    def came(side, h):
        c = z - h if side == 0 else z + h
        return pltpu.make_async_remote_copy(
            src_ref=cot_ref.at[c],
            dst_ref=cot_ref.at[c],
            send_sem=hsend.at[side, h],
            recv_sem=hrecv.at[side, h],
            device_id=toward(side),
            device_id_type=MESH,
        )

    def add(side, s, q):
        d = goal(side, s)

        @pl.loop(q * size, (q + 1) * size)
        def _(j):
            here = sums[side, d, j].astype(jnp.float32) + part_ref[d, j].astype(jnp.float32)
            sums[side, d, j] = here.astype(sums.dtype)

    for s in range(far - 1):
        for q in range(chunks):
            for side in range(2):
                pl.when(where(side) == 0)(lambda: summed(side, s, True, q).start())
                if s:

                    @pl.when((where(side) > 0) & (where(side) <= s))
                    def _():
                        arrived(side, s - 1, q).wait_recv()
                        add(side, s, q)
                        summed(side, s, False, q).start()

        h = s + 2
        if h < far:
            for side in range(2):
                if h > 2:
                    pl.when(where(side) >= h - 1)(lambda: came(side, h - 1).wait_recv())
                active = (where(side) >= h - 1) & (where(side) < far - 1)
                pl.when(active)(lambda: passed(side, h).start())

    for q in range(chunks):
        for side in range(2):
            pl.when(where(side) > 0)(lambda: arrived(side, far - 2, q).wait_recv())

        @pl.loop(q * size, (q + 1) * size)
        def _(j):
            here = part_ref[z, j].astype(jnp.float32)
            up = jnp.where(z > 0, sums[0, z, j].astype(jnp.float32), 0.0)
            down = jnp.where(z < far - 1, sums[1, z, j].astype(jnp.float32), 0.0)
            total[j] = (here + up + down).astype(total.dtype)

        for j in range(q * size, (q + 1) * size):
            pl.when(mine != j)(lambda: give(j).start())

    out_ref[:, columns(mine, part)] = total[mine]
    for j in range(total.shape[0]):
        pl.when(mine != j)(lambda: give(j).wait_send())
        pl.when(mine != j)(lambda: given(j).wait_recv())
    for side in range(2):
        for s in range(far - 1):
            for q in range(chunks):
                pl.when(where(side) == 0)(lambda: summed(side, s, True, q).wait_send())
                if s:
                    busy = (where(side) > 0) & (where(side) <= s)
                    pl.when(busy)(lambda: summed(side, s, False, q).wait_send())
        for h in range(2, far):
            active = (where(side) >= h - 1) & (where(side) < far - 1)
            pl.when(active)(lambda: passed(side, h).wait_send())
        if far > 2:
            pl.when(where(side) >= far - 1)(lambda: came(side, far - 1).wait_recv())
    for k in range(3):
        pl.when(inside[k])(lambda k=k: keep(k).wait())


def table_kernel(sizes, send_ref, who_ref, out_ref, whose_ref, send_sem, recv_sem):
    me = place()
    half = send_ref.shape[2] // 2
    greet([moved(me, sizes, s) for s in steps(sizes)])
    out_ref[me[0], me[1], me[2], me[3]] = send_ref[me[0]]
    whose_ref[me[0], me[1], me[2], me[3]] = who_ref[me[0]]
    started = []

    def own(item, axis, peer):
        if item == 0:
            return who_ref.at[peer[0]]
        return send_ref.at[peer[0], :, pl.ds((item - 1) * half, half)]

    def slot(item, spot):
        if item == 0:
            return whose_ref.at[spot[0], spot[1], spot[2], spot[3]]
        return out_ref.at[spot[0], spot[1], spot[2], spot[3], :, pl.ds((item - 1) * half, half)]

    plans = [tree(order, sizes) for order in ORDERS[:1] + ORDERS]
    spread(me, sizes, plans, own, slot, started, send_sem, recv_sem)
    for copy in started:
        copy.wait_send()


VMEM = pl.BlockSpec(memory_space=pltpu.VMEM)


def gather(sizes, mine, values, cotangent, near, part):
    layer = near * sizes[3]
    count = sizes[0] * sizes[1] * sizes[2] * sizes[3]
    return pl.pallas_call(
        functools.partial(gather_kernel, sizes),
        out_shape=(
            jax.ShapeDtypeStruct(sizes + (2, mine.shape[0] // 2, mine.shape[1]), mine.dtype),
            jax.ShapeDtypeStruct((near, values.shape[0], part), values.dtype),
            jax.ShapeDtypeStruct((3, layer, cotangent.shape[0], part), cotangent.dtype),
        ),
        in_specs=[VMEM] * 3,
        out_specs=(VMEM, VMEM, VMEM),
        scratch_shapes=[
            pltpu.SemaphoreType.DMA((2, count)),
            pltpu.SemaphoreType.DMA((2, count)),
            pltpu.SemaphoreType.DMA((3,)),
            pltpu.SemaphoreType.DMA((3,)),
            pltpu.SemaphoreType.DMA((layer,)),
            pltpu.SemaphoreType.DMA((layer,)),
            pltpu.SemaphoreType.DMA((2,)),
            pltpu.SemaphoreType.DMA((2,)),
            pltpu.SemaphoreType.DMA,
        ],
        compiler_params=pltpu.CompilerParams(collective_id=0, has_side_effects=True),
        name="gather_rows",
    )(mine, values, cotangent)


def push(sizes, grad):
    layer, rows, part = grad.shape
    return pl.pallas_call(
        functools.partial(push_kernel, sizes),
        out_shape=jax.ShapeDtypeStruct((rows, layer * part), grad.dtype),
        in_specs=[VMEM],
        out_specs=VMEM,
        scratch_shapes=[pltpu.SemaphoreType.DMA((layer,)), pltpu.SemaphoreType.DMA((layer,))],
        compiler_params=pltpu.CompilerParams(collective_id=2, has_side_effects=True),
        name="push_gradient",
    )(grad)


def line(sizes, partial, hops):
    far, layer, rows, part = partial.shape
    return pl.pallas_call(
        functools.partial(line_kernel, sizes),
        out_shape=(
            jax.ShapeDtypeStruct((rows, layer * part), partial.dtype),
            jax.ShapeDtypeStruct((far,) + hops.shape[1:], hops.dtype),
        ),
        in_specs=[VMEM] * 2,
        out_specs=(VMEM, VMEM),
        scratch_shapes=[
            pltpu.VMEM((2,) + partial.shape, partial.dtype),
            pltpu.VMEM(partial.shape[1:], partial.dtype),
            pltpu.SemaphoreType.DMA((2, far, CHUNKS)),
            pltpu.SemaphoreType.DMA((2, far, CHUNKS)),
            pltpu.SemaphoreType.DMA((2, far)),
            pltpu.SemaphoreType.DMA((2, far)),
            pltpu.SemaphoreType.DMA((layer,)),
            pltpu.SemaphoreType.DMA((layer,)),
            pltpu.SemaphoreType.DMA((3,)),
        ],
        compiler_params=pltpu.CompilerParams(collective_id=3, has_side_effects=True),
        name="sum_line",
    )(partial, hops)


def exchange(sizes, send, who):
    count = sizes[0] * sizes[1] * sizes[2] * sizes[3]
    return pl.pallas_call(
        functools.partial(table_kernel, sizes),
        out_shape=(
            jax.ShapeDtypeStruct(sizes + send.shape[1:], send.dtype),
            jax.ShapeDtypeStruct(sizes + who.shape[1:], who.dtype),
        ),
        in_specs=[VMEM] * 2,
        out_specs=(VMEM, VMEM),
        scratch_shapes=[
            pltpu.SemaphoreType.DMA((3, count)),
            pltpu.SemaphoreType.DMA((3, count)),
        ],
        compiler_params=pltpu.CompilerParams(collective_id=1, has_side_effects=True),
        name="exchange_tables",
    )(send, who)


def body(tokens, owner, row_pick, query_weight, sub_keys, values, cotangent):
    tok_rows = tokens.shape[0]
    heads = owner.shape[1]
    width = tokens.shape[1]
    block_rows = values.shape[0]
    key_width = sub_keys.shape[2]
    far = lax.axis_size("far")
    near = lax.axis_size("near")
    copies = lax.axis_size("dp")
    groups = far * near
    layer = near * copies
    part = width // layer
    capacity = max(2, 3 * tok_rows * heads // (2 * groups))
    requests = tok_rows * heads
    f32, bf16 = jnp.float32, jnp.bfloat16
    y = lax.axis_index("dp")

    own = query_weight.shape[0] // copies
    mine = lax.dynamic_slice_in_dim(query_weight, y * own, own, axis=0)
    sizes = (far, 2, near // 2, copies)
    qw, vals, hops = gather(sizes, mine, values, cotangent, near, part)
    qw = qw.reshape(width, -1)
    query = jnp.dot(tokens, qw, preferred_element_type=f32).astype(bf16)
    query = query.reshape(tok_rows, heads, key_width)
    full = jnp.einsum("thk,hrk->thr", query, sub_keys, preferred_element_type=f32)
    match = row_pick[:, :, :, None] == jnp.arange(block_rows, dtype=jnp.int32)[None, None, None, :]
    score = jnp.where(jnp.any(match, axis=2), full * (1.0 / key_width**0.5), -jnp.inf)
    top = jnp.max(score, axis=2, keepdims=True)
    expo = jnp.exp(score - top)
    weight = (expo / jnp.sum(expo, axis=2, keepdims=True)).astype(bf16)
    table = weight.reshape(requests, block_rows)

    ids = jnp.arange(groups, dtype=jnp.int32)
    hits = owner[:, :, None] == ids[None, None, :]
    named = jnp.any(hits, axis=1)
    row = jnp.arange(tok_rows, dtype=jnp.int32)
    before = (row[:, None] > row[None, :]).astype(bf16)
    rank = jnp.dot(before, named.astype(bf16), preferred_element_type=f32).astype(jnp.int32)
    places = jnp.arange(capacity, dtype=jnp.int32)
    own_slot = hits & (rank[:, None, :] < capacity)
    slot = jnp.sum(jnp.where(own_slot, ids * capacity + rank[:, None, :], 0), axis=2).reshape(-1)
    dispatch = (
        jnp.arange(groups * capacity, dtype=jnp.int32)[:, None] == slot[None, :]
    ).astype(bf16)
    send = jnp.dot(dispatch, table, preferred_element_type=f32).astype(bf16)
    send = send.reshape(groups, capacity, block_rows)
    held = named[:, :, None] & (rank[:, :, None] == places)
    who = jnp.sum(jnp.where(held, row[:, None, None] + 1, 0), axis=0) - 1
    lanes = 128 * -(-capacity // 128)
    who = who.astype(bf16).reshape(far, near, capacity)
    who = jnp.pad(who, ((0, 0), (0, 16 * -(-near // 16) - near), (0, lanes - capacity)))
    slots, who = exchange(sizes, send.reshape(far, near * capacity, block_rows), who)
    slots = slots.reshape(far * layer, near, capacity, block_rows)
    who = who.reshape((far * layer,) + who.shape[4:])[:, :near, :capacity]
    pick = (who[:, None, :, :] == row.astype(bf16)[None, :, None, None]).astype(bf16)
    pick = pick.reshape(far * layer, tok_rows, near * capacity)

    reads = jnp.einsum("dlcr,lrw->dlcw", slots, vals, preferred_element_type=f32).astype(bf16)
    reads = reads.reshape(far * layer, near * capacity, part)
    partial = jnp.einsum("dts,dsw->dtw", pick, reads, preferred_element_type=f32).astype(bf16)
    partial = partial.reshape(far, layer, tok_rows, part)
    memory_out, cot = line(sizes, partial, hops)
    cot = cot.reshape(far * layer, tok_rows, part)

    terms = jnp.einsum("dts,dtw->dsw", pick, cot, preferred_element_type=f32).astype(bf16)
    terms = terms.reshape(far * layer, near, capacity, part)
    grad = jnp.einsum("dlcr,dlcw->lrw", slots, terms, preferred_element_type=f32).astype(bf16)
    grad = grad.reshape(layer, block_rows // copies, part)
    grad_values = push(sizes, grad)
    return memory_out, grad_values


def solution(mesh):
    fsdp, dp = mesh.shape["fsdp"], mesh.shape["dp"]
    fine = Mesh(mesh.devices.reshape(fsdp // INNER, INNER, dp), ("far", "near", "dp"))
    rows, held = ("far", "near", "dp"), ("far", "near")
    placed = (
        P(rows, None),
        P(rows, None),
        P(rows, None, None),
        P(held, None),
        P(),
        P(held, None),
        P(rows, None),
    )
    return jax.shard_map(
        body,
        mesh=fine,
        in_specs=placed,
        out_specs=(P(rows, None), P(rows, None)),
        check_vma=False,
    )
```

```python
import functools
import jax
import jax.numpy as jnp
from jax import lax
from jax.experimental import pallas as pl
from jax.experimental.pallas import tpu as pltpu
from jax.sharding import Mesh, PartitionSpec as P

INNER = 4
CHUNKS = 4
MESH = pl.DeviceIdType.MESH
AXES = ("far", "high", "low", "dp")
ORDERS = (("far", "dp", "high", "low"), ("far", "high", "dp", "low"))


def place():
    near = lax.axis_index("near")
    return (lax.axis_index("far"), near // 2, near % 2, lax.axis_index("dp"))


def moved(me, sizes, off):
    return tuple(lax.rem(m + o, n) if o else m for m, o, n in zip(me, off, sizes))


def device(spot):
    return {"far": spot[0], "near": spot[1] * 2 + spot[2], "dp": spot[3]}


def tree(order, sizes):
    nodes = [((0, 0, 0, 0), -1, [])]
    for off, stage, copies in nodes:
        for k in range(stage + 1, len(order)):
            axis = AXES.index(order[k])
            for r in range(1, sizes[axis]):
                child = list(off)
                child[axis] = (child[axis] - r) % sizes[axis]
                copies.append((axis, r, len(nodes)))
                nodes.append((tuple(child), k, []))
    return nodes


def greet(peers):
    barrier = pltpu.get_barrier_semaphore()
    for spot in peers:
        pl.semaphore_signal(barrier, inc=1, device_id=device(spot), device_id_type=MESH)
    pl.semaphore_wait(barrier, len(peers))


def steps(sizes):
    found = []
    for axis, n in enumerate(sizes):
        for r in range(1, n):
            found.append(tuple(r if a == axis else 0 for a in range(4)))
    return found


def spread(me, sizes, plans, own, slot, started, send_sem, recv_sem, events=()):
    pending = {}
    longest = max(len(nodes) for nodes in plans)
    for number in range(longest):
        for when, event in events:
            if when == number:
                event()
        for item, nodes in enumerate(plans):
            if number >= len(nodes):
                continue
            off, stage, copies = nodes[number]
            if number:
                pending[item, number].wait_recv()
            here = moved(me, sizes, off)
            for axis, r, child in copies:
                step = tuple(r if a == axis else 0 for a in range(4))
                peer = moved(me, sizes, step)
                copy = pltpu.make_async_remote_copy(
                    src_ref=slot(item, here) if number else own(item, axis, peer),
                    dst_ref=slot(item, here),
                    send_sem=send_sem.at[item, child],
                    recv_sem=recv_sem.at[item, child],
                    device_id=device(peer),
                    device_id_type=MESH,
                )
                copy.start()
                pending[item, child] = copy
                started.append(copy)


def rank_in_layer(spot, sizes):
    return (spot[1] * 2 + spot[2]) * sizes[3] + spot[3]


def layer_peers(me, sizes):
    layer = sizes[1] * sizes[2] * sizes[3]
    mine = rank_in_layer(me, sizes)
    for r in range(1, layer):
        j = lax.rem(mine + r, layer)
        near = j // sizes[3]
        yield r - 1, j, (me[0], near // 2, near % 2, lax.rem(j, sizes[3]))


def columns(j, part):
    return pl.ds(pl.multiple_of(j * part, part), part)


def gather_kernel(
    sizes, qw_ref, val_ref, cot_ref, out_ref, vals_ref, hop_ref,
    send_sem, recv_sem, vsend, vrecv, csend, crecv, hsend, hrecv, local,
):
    me = place()
    far = sizes[0]
    z = me[0]
    mine = rank_in_layer(me, sizes)
    width = hop_ref.shape[3]
    half = qw_ref.shape[0] // 2
    part = vals_ref.shape[2]
    corner = (0, 1, 1, 0)
    beside = [moved(me, sizes, s) for s in steps((far, 1, 1, 1))]
    greet(beside + [spot for _, _, spot in layer_peers(me, sizes)])
    for item in range(2):
        out_ref[me[0], me[1], me[2], me[3], item] = qw_ref[pl.ds(item * half, half), :]
    started = []

    def own(item, axis, peer):
        return qw_ref.at[pl.ds(item * half, half), :]

    def slot(item, spot):
        return out_ref.at[spot[0], spot[1], spot[2], spot[3], item]

    cuts = []

    def hop(side):
        return pltpu.make_async_remote_copy(
            src_ref=hop_ref.at[0],
            dst_ref=hop_ref.at[1 + side],
            send_sem=hsend.at[side],
            recv_sem=hrecv.at[side],
            device_id=device((z + 1 - 2 * side,) + me[1:]),
            device_id_type=MESH,
        )

    def cut():
        for number, j, spot in layer_peers(me, sizes):
            copy = pltpu.make_async_remote_copy(
                src_ref=cot_ref.at[:, columns(j, width)],
                dst_ref=hop_ref.at[0, mine],
                send_sem=csend.at[number],
                recv_sem=crecv.at[number],
                device_id=device(spot),
                device_id_type=MESH,
            )
            copy.start()
            cuts.append(copy)
        keep = pltpu.make_async_copy(
            cot_ref.at[:, columns(mine, width)], hop_ref.at[0, mine], local
        )
        keep.start()
        cuts.append(keep)

    def forward():
        for copy in cuts[:-1]:
            copy.wait_recv()
        cuts[-1].wait()
        pl.when(z < far - 1)(lambda: hop(0).start())
        pl.when(z > 0)(lambda: hop(1).start())

    pushes = []

    def slices():
        for number, step in enumerate(((0, 1, 0, 0), (0, 0, 1, 0), corner)):
            peer = moved(me, sizes, step)
            first = ((peer[1] * 2 + peer[2]) * sizes[3] + peer[3]) * part
            copy = pltpu.make_async_remote_copy(
                src_ref=val_ref.at[:, pl.ds(pl.multiple_of(first, part), part)],
                dst_ref=vals_ref.at[me[1] * 2 + me[2]],
                send_sem=vsend.at[number],
                recv_sem=vrecv.at[number],
                device_id=device(peer),
                device_id_type=MESH,
            )
            copy.start()
            pushes.append(copy)

    plans = [tree(order, sizes) for order in ORDERS]
    events = ((1, cut), (12, forward), (14, slices))
    spread(me, sizes, plans, own, slot, started, send_sem, recv_sem, events)
    started.extend(cuts[:-1])
    first = ((me[1] * 2 + me[2]) * sizes[3] + me[3]) * part
    vals_ref[me[1] * 2 + me[2]] = val_ref[:, pl.ds(pl.multiple_of(first, part), part)]
    for copy in started:
        copy.wait_send()
    for copy in pushes:
        copy.wait()
    pl.when(z < far - 1)(lambda: hop(0).wait_send())
    pl.when(z > 0)(lambda: hop(0).wait_recv())
    pl.when(z > 0)(lambda: hop(1).wait_send())
    pl.when(z < far - 1)(lambda: hop(1).wait_recv())


def push_layer(me, sizes, source, target, send_sem, recv_sem):
    mine = rank_in_layer(me, sizes)
    part = source.shape[2]
    copies = []
    for number, j, spot in layer_peers(me, sizes):
        copy = pltpu.make_async_remote_copy(
            src_ref=source.at[j],
            dst_ref=target.at[:, columns(mine, part)],
            send_sem=send_sem.at[number],
            recv_sem=recv_sem.at[number],
            device_id=device(spot),
            device_id_type=MESH,
        )
        copy.start()
        copies.append(copy)
    target[:, columns(mine, part)] = source[mine]
    for copy in copies:
        copy.wait()


def push_kernel(sizes, grad_ref, out_ref, send_sem, recv_sem):
    me = place()
    greet([spot for _, _, spot in layer_peers(me, sizes)])
    push_layer(me, sizes, grad_ref, out_ref, send_sem, recv_sem)


def line_kernel(
    sizes, part_ref, hop_ref, out_ref, cot_ref, sums, total,
    ssend, srecv, hsend, hrecv, csend, crecv, local,
):
    me = place()
    far = sizes[0]
    z = me[0]
    beside = [moved(me, sizes, s) for s in steps((far, 1, 1, 1))]
    greet(beside + [spot for _, _, spot in layer_peers(me, sizes)])
    near = ((0, z), (1, z - 1), (2, z + 1))
    inside = (z >= 0, z > 0, z < far - 1)

    def keep(k):
        return pltpu.make_async_copy(hop_ref.at[k], cot_ref.at[near[k][1]], local.at[k])

    for k in range(3):
        pl.when(inside[k])(lambda k=k: keep(k).start())

    chunks = ssend.shape[2]
    size = total.shape[0] // chunks
    mine = rank_in_layer(me, sizes)
    part = total.shape[2]

    def chunk(q):
        return pl.ds(q * size, size)

    def give(j):
        near, y = j // sizes[3], j % sizes[3]
        return pltpu.make_async_remote_copy(
            src_ref=total.at[j],
            dst_ref=out_ref.at[:, columns(mine, part)],
            send_sem=csend.at[j],
            recv_sem=crecv.at[mine],
            device_id=device((z, near // 2, near % 2, y)),
            device_id_type=MESH,
        )

    def given(j):
        return pltpu.make_async_remote_copy(
            src_ref=total.at[j],
            dst_ref=out_ref.at[:, columns(j, part)],
            send_sem=csend.at[j],
            recv_sem=crecv.at[j],
            device_id=device((z, (j // sizes[3]) // 2, (j // sizes[3]) % 2, j % sizes[3])),
            device_id_type=MESH,
        )

    def where(side):
        return z if side == 0 else far - 1 - z

    def toward(side):
        return device((z + 1 - 2 * side,) + me[1:])

    def goal(side, s):
        return far - 1 - s + z if side == 0 else s - far + 1 + z

    def summed(side, s, first, q):
        d = goal(side, s)
        return pltpu.make_async_remote_copy(
            src_ref=part_ref.at[d, chunk(q)] if first else sums.at[side, d, chunk(q)],
            dst_ref=sums.at[side, d, chunk(q)],
            send_sem=ssend.at[side, s, q],
            recv_sem=srecv.at[side, s, q],
            device_id=toward(side),
            device_id_type=MESH,
        )

    def arrived(side, s, q):
        d = goal(side, s + 1)
        return pltpu.make_async_remote_copy(
            src_ref=sums.at[side, d, chunk(q)],
            dst_ref=sums.at[side, d, chunk(q)],
            send_sem=ssend.at[side, s, q],
            recv_sem=srecv.at[side, s, q],
            device_id=toward(side),
            device_id_type=MESH,
        )

    def passed(side, h):
        c = z - (h - 1) if side == 0 else z + (h - 1)
        return pltpu.make_async_remote_copy(
            src_ref=hop_ref.at[1 + side] if h == 2 else cot_ref.at[c],
            dst_ref=cot_ref.at[c],
            send_sem=hsend.at[side, h],
            recv_sem=hrecv.at[side, h],
            device_id=toward(side),
            device_id_type=MESH,
        )

    def came(side, h):
        c = z - h if side == 0 else z + h
        return pltpu.make_async_remote_copy(
            src_ref=cot_ref.at[c],
            dst_ref=cot_ref.at[c],
            send_sem=hsend.at[side, h],
            recv_sem=hrecv.at[side, h],
            device_id=toward(side),
            device_id_type=MESH,
        )

    def add(side, s, q):
        d = goal(side, s)

        @pl.loop(q * size, (q + 1) * size)
        def _(j):
            here = sums[side, d, j].astype(jnp.float32) + part_ref[d, j].astype(jnp.float32)
            sums[side, d, j] = here.astype(sums.dtype)

    for s in range(far - 1):
        for q in range(chunks):
            for side in range(2):
                pl.when(where(side) == 0)(lambda: summed(side, s, True, q).start())
                if s:

                    @pl.when((where(side) > 0) & (where(side) <= s))
                    def _():
                        arrived(side, s - 1, q).wait_recv()
                        add(side, s, q)
                        summed(side, s, False, q).start()

        h = s + 2
        if h < far:
            for side in range(2):
                if h > 2:
                    pl.when(where(side) >= h - 1)(lambda: came(side, h - 1).wait_recv())
                active = (where(side) >= h - 1) & (where(side) < far - 1)
                pl.when(active)(lambda: passed(side, h).start())

    for q in range(chunks):
        for side in range(2):
            pl.when(where(side) > 0)(lambda: arrived(side, far - 2, q).wait_recv())

        @pl.loop(q * size, (q + 1) * size)
        def _(j):
            here = part_ref[z, j].astype(jnp.float32)
            up = jnp.where(z > 0, sums[0, z, j].astype(jnp.float32), 0.0)
            down = jnp.where(z < far - 1, sums[1, z, j].astype(jnp.float32), 0.0)
            total[j] = (here + up + down).astype(total.dtype)

        for j in range(q * size, (q + 1) * size):
            pl.when(mine != j)(lambda: give(j).start())

    out_ref[:, columns(mine, part)] = total[mine]
    for j in range(total.shape[0]):
        pl.when(mine != j)(lambda: give(j).wait_send())
        pl.when(mine != j)(lambda: given(j).wait_recv())
    for side in range(2):
        for s in range(far - 1):
            for q in range(chunks):
                pl.when(where(side) == 0)(lambda: summed(side, s, True, q).wait_send())
                if s:
                    busy = (where(side) > 0) & (where(side) <= s)
                    pl.when(busy)(lambda: summed(side, s, False, q).wait_send())
        for h in range(2, far):
            active = (where(side) >= h - 1) & (where(side) < far - 1)
            pl.when(active)(lambda: passed(side, h).wait_send())
        if far > 2:
            pl.when(where(side) >= far - 1)(lambda: came(side, far - 1).wait_recv())
    for k in range(3):
        pl.when(inside[k])(lambda k=k: keep(k).wait())


def table_kernel(sizes, send_ref, who_ref, out_ref, whose_ref, send_sem, recv_sem):
    me = place()
    half = send_ref.shape[2] // 2
    greet([moved(me, sizes, s) for s in steps(sizes)])
    out_ref[me[0], me[1], me[2], me[3]] = send_ref[me[0]]
    whose_ref[me[0], me[1], me[2], me[3]] = who_ref[me[0]]
    started = []

    def own(item, axis, peer):
        if item == 0:
            return who_ref.at[peer[0]]
        return send_ref.at[peer[0], :, pl.ds((item - 1) * half, half)]

    def slot(item, spot):
        if item == 0:
            return whose_ref.at[spot[0], spot[1], spot[2], spot[3]]
        return out_ref.at[spot[0], spot[1], spot[2], spot[3], :, pl.ds((item - 1) * half, half)]

    plans = [tree(order, sizes) for order in ORDERS[:1] + ORDERS]
    spread(me, sizes, plans, own, slot, started, send_sem, recv_sem)
    for copy in started:
        copy.wait_send()


VMEM = pl.BlockSpec(memory_space=pltpu.VMEM)


def gather(sizes, mine, values, cotangent, near, part):
    layer = near * sizes[3]
    count = sizes[0] * sizes[1] * sizes[2] * sizes[3]
    return pl.pallas_call(
        functools.partial(gather_kernel, sizes),
        out_shape=(
            jax.ShapeDtypeStruct(sizes + (2, mine.shape[0] // 2, mine.shape[1]), mine.dtype),
            jax.ShapeDtypeStruct((near, values.shape[0], part), values.dtype),
            jax.ShapeDtypeStruct((3, layer, cotangent.shape[0], part), cotangent.dtype),
        ),
        in_specs=[VMEM] * 3,
        out_specs=(VMEM, VMEM, VMEM),
        scratch_shapes=[
            pltpu.SemaphoreType.DMA((2, count)),
            pltpu.SemaphoreType.DMA((2, count)),
            pltpu.SemaphoreType.DMA((3,)),
            pltpu.SemaphoreType.DMA((3,)),
            pltpu.SemaphoreType.DMA((layer,)),
            pltpu.SemaphoreType.DMA((layer,)),
            pltpu.SemaphoreType.DMA((2,)),
            pltpu.SemaphoreType.DMA((2,)),
            pltpu.SemaphoreType.DMA,
        ],
        compiler_params=pltpu.CompilerParams(collective_id=0, has_side_effects=True),
        name="gather_rows",
    )(mine, values, cotangent)


def push(sizes, grad):
    layer, rows, part = grad.shape
    return pl.pallas_call(
        functools.partial(push_kernel, sizes),
        out_shape=jax.ShapeDtypeStruct((rows, layer * part), grad.dtype),
        in_specs=[VMEM],
        out_specs=VMEM,
        scratch_shapes=[pltpu.SemaphoreType.DMA((layer,)), pltpu.SemaphoreType.DMA((layer,))],
        compiler_params=pltpu.CompilerParams(collective_id=2, has_side_effects=True),
        name="push_gradient",
    )(grad)


def line(sizes, partial, hops):
    far, layer, rows, part = partial.shape
    return pl.pallas_call(
        functools.partial(line_kernel, sizes),
        out_shape=(
            jax.ShapeDtypeStruct((rows, layer * part), partial.dtype),
            jax.ShapeDtypeStruct((far,) + hops.shape[1:], hops.dtype),
        ),
        in_specs=[VMEM] * 2,
        out_specs=(VMEM, VMEM),
        scratch_shapes=[
            pltpu.VMEM((2,) + partial.shape, partial.dtype),
            pltpu.VMEM(partial.shape[1:], partial.dtype),
            pltpu.SemaphoreType.DMA((2, far, CHUNKS)),
            pltpu.SemaphoreType.DMA((2, far, CHUNKS)),
            pltpu.SemaphoreType.DMA((2, far)),
            pltpu.SemaphoreType.DMA((2, far)),
            pltpu.SemaphoreType.DMA((layer,)),
            pltpu.SemaphoreType.DMA((layer,)),
            pltpu.SemaphoreType.DMA((3,)),
        ],
        compiler_params=pltpu.CompilerParams(collective_id=3, has_side_effects=True),
        name="sum_line",
    )(partial, hops)


def exchange(sizes, send, who):
    count = sizes[0] * sizes[1] * sizes[2] * sizes[3]
    return pl.pallas_call(
        functools.partial(table_kernel, sizes),
        out_shape=(
            jax.ShapeDtypeStruct(sizes + send.shape[1:], send.dtype),
            jax.ShapeDtypeStruct(sizes + who.shape[1:], who.dtype),
        ),
        in_specs=[VMEM] * 2,
        out_specs=(VMEM, VMEM),
        scratch_shapes=[
            pltpu.SemaphoreType.DMA((3, count)),
            pltpu.SemaphoreType.DMA((3, count)),
        ],
        compiler_params=pltpu.CompilerParams(collective_id=1, has_side_effects=True),
        name="exchange_tables",
    )(send, who)


def body(tokens, owner, row_pick, query_weight, sub_keys, values, cotangent):
    tok_rows = tokens.shape[0]
    heads = owner.shape[1]
    width = tokens.shape[1]
    block_rows = values.shape[0]
    key_width = sub_keys.shape[2]
    far = lax.axis_size("far")
    near = lax.axis_size("near")
    copies = lax.axis_size("dp")
    groups = far * near
    layer = near * copies
    part = width // layer
    capacity = max(2, 3 * tok_rows * heads // (2 * groups))
    requests = tok_rows * heads
    f32, bf16 = jnp.float32, jnp.bfloat16
    y = lax.axis_index("dp")

    own = query_weight.shape[0] // copies
    mine = lax.dynamic_slice_in_dim(query_weight, y * own, own, axis=0)
    sizes = (far, 2, near // 2, copies)
    qw, vals, hops = gather(sizes, mine, values, cotangent, near, part)
    qw = qw.reshape(width, -1)
    query = jnp.dot(tokens, qw, preferred_element_type=f32).astype(bf16)
    query = query.reshape(tok_rows, heads, key_width)
    full = jnp.einsum("thk,hrk->thr", query, sub_keys, preferred_element_type=f32)
    match = row_pick[:, :, :, None] == jnp.arange(block_rows, dtype=jnp.int32)[None, None, None, :]
    score = jnp.where(jnp.any(match, axis=2), full * (1.0 / key_width**0.5), -jnp.inf)
    top = jnp.max(score, axis=2, keepdims=True)
    expo = jnp.exp(score - top)
    weight = (expo / jnp.sum(expo, axis=2, keepdims=True)).astype(bf16)
    table = weight.reshape(requests, block_rows)

    ids = jnp.arange(groups, dtype=jnp.int32)
    hits = owner[:, :, None] == ids[None, None, :]
    named = jnp.any(hits, axis=1)
    row = jnp.arange(tok_rows, dtype=jnp.int32)
    before = (row[:, None] > row[None, :]).astype(bf16)
    rank = jnp.dot(before, named.astype(bf16), preferred_element_type=f32).astype(jnp.int32)
    places = jnp.arange(capacity, dtype=jnp.int32)
    own_slot = hits & (rank[:, None, :] < capacity)
    slot = jnp.sum(jnp.where(own_slot, ids * capacity + rank[:, None, :], 0), axis=2).reshape(-1)
    dispatch = (
        jnp.arange(groups * capacity, dtype=jnp.int32)[:, None] == slot[None, :]
    ).astype(bf16)
    send = jnp.dot(dispatch, table, preferred_element_type=f32).astype(bf16)
    send = send.reshape(groups, capacity, block_rows)
    held = named[:, :, None] & (rank[:, :, None] == places)
    who = jnp.sum(jnp.where(held, row[:, None, None] + 1, 0), axis=0) - 1
    lanes = 128 * -(-capacity // 128)
    who = who.astype(bf16).reshape(far, near, capacity)
    who = jnp.pad(who, ((0, 0), (0, 16 * -(-near // 16) - near), (0, lanes - capacity)))
    slots, who = exchange(sizes, send.reshape(far, near * capacity, block_rows), who)
    slots = slots.reshape(far * layer, near, capacity, block_rows)
    who = who.reshape((far * layer,) + who.shape[4:])[:, :near, :capacity]
    pick = (who[:, None, :, :] == row.astype(bf16)[None, :, None, None]).astype(bf16)
    pick = pick.reshape(far * layer, tok_rows, near * capacity)

    reads = jnp.einsum("dlcr,lrw->dlcw", slots, vals, preferred_element_type=f32).astype(bf16)
    reads = reads.reshape(far * layer, near * capacity, part)
    partial = jnp.einsum("dts,dsw->dtw", pick, reads, preferred_element_type=f32).astype(bf16)
    partial = partial.reshape(far, layer, tok_rows, part)
    memory_out, cot = line(sizes, partial, hops)
    cot = cot.reshape(far * layer, tok_rows, part)

    terms = jnp.einsum("dts,dtw->dsw", pick, cot, preferred_element_type=f32).astype(bf16)
    terms = terms.reshape(far * layer, near, capacity, part)
    grad = jnp.einsum("dlcr,dlcw->lrw", slots, terms, preferred_element_type=f32).astype(bf16)
    grad = grad.reshape(layer, block_rows // copies, part)
    grad_values = push(sizes, grad)
    return memory_out, grad_values


def solution(mesh):
    fsdp, dp = mesh.shape["fsdp"], mesh.shape["dp"]
    fine = Mesh(mesh.devices.reshape(fsdp // INNER, INNER, dp), ("far", "near", "dp"))
    rows, held = ("far", "near", "dp"), ("far", "near")
    placed = (
        P(rows, None),
        P(rows, None),
        P(rows, None, None),
        P(held, None),
        P(),
        P(held, None),
        P(rows, None),
    )
    return jax.shard_map(
        body,
        mesh=fine,
        in_specs=placed,
        out_specs=(P(rows, None), P(rows, None)),
        check_vma=False,
    )
```
